32 devices in a mesh: pole: 2 (over y), col: 4 (over z), row: 4 (over x, core).
Axes of the slice: x: 2, y: 2, z: 4, core: 2. Of those that a mesh axis runs over, the one named last changes fastest.
Arguments:
- ancestor_inverse: bfloat16 [4, 2048, 2048], P('pole', 'col', 'row'), parts along dimension 0, may hold values from -0.125 to 0.125
- panels: bfloat16 [6, 2048, 512], P('pole', 'col'), parts along dimension 0, may hold values from -0.8984375 to 0.8984375
- block_lists: int32 [6, 16], P('pole'), parts along dimension 0, may hold values from -1 to 15, as said below
- diag_inverse: float32 [6, 256, 512], P('pole', ('col', 'row')), parts along dimension 0, may hold values from -6 to 6
Outputs:
- offdiag: bfloat16 [6, 2048, 512], P('pole', ('col', 'row')), parts along dimension 0
- diag_block: float32 [6, 256, 512], P('pole', ('col', 'row')), parts along dimension 0
The draws below stay inside these ranges and needn't reach their ends.
There are 2 independent parts, one for each index of `pole`. The reference program is written for one: setup_inputs(seed, part) draws one part's arguments, and reference() takes and returns one part's arrays. A program takes and returns all parts, laid end to end along the dimension named above; each array names one. Nothing has to cross between parts.
Inputs may be any that keep to these rules, and one draw needn't show every extreme that they name: `block_lists`: in every supernode, the slots of range r hold distinct blocks of r * 4 to r * 4 + 3, filled slots first and -1 after them; every range has at least one filled slot, and some range has all 4 filled.
All inputs are finite; a program needn't handle non-finite values.
Results may differ from the reference program's by a relative error of at most 0.017.
Values may be sent and summed in bfloat16 or wider, within the bound.
No kernel may reach another device: no remote copies, remote signals or barrier semaphores. Data moves between devices by JAX's collectives and lax.ppermute only.
A program may use at most 64 MiB of HBM per device.

```python
import jax
import jax.numpy as jnp
from jax import lax

W = 256
BS = 128
BPR = 4
CAP = 4
NSUP = 3
GRID = 4
M = 2048
SLOTS = 16


def draw_block_lists(key, part):
    key_count = jax.random.fold_in(key, 11)
    key_full = jax.random.fold_in(key, 12)
    key_order = jax.random.fold_in(key, 13)
    counts = jax.random.randint(key_count, (NSUP, GRID), 1, CAP + 1)
    full_range = jax.random.randint(key_full, (NSUP,), 0, GRID)
    ranges = jnp.arange(GRID, dtype=jnp.int32)
    counts = jnp.where(ranges[None, :] == full_range[:, None], CAP, counts)
    scores = jax.random.randint(key_order, (NSUP, GRID, BPR), 0, 1 << 20) * BPR + jnp.arange(BPR, dtype=jnp.int32)[None, None, :]
    order = jnp.argsort(scores, axis=2)[:, :, :CAP].astype(jnp.int32)
    blocks = ranges[None, :, None] * BPR + order
    slot_ids = jnp.arange(CAP, dtype=jnp.int32)
    filled = jnp.where(slot_ids[None, None, :] < counts[:, :, None], blocks, -1)
    return filled.reshape(NSUP, GRID * CAP).astype(jnp.int32)


def block_scale(stream_key, shape, split, low, largest):
    gain = 1.0
    for axis_at, parts in split:
        steps = jax.random.uniform(jax.random.fold_in(jax.random.fold_in(stream_key, 6), axis_at), (parts,), jnp.float32, low / len(split), largest / len(split))
        gain = gain * jnp.repeat(jnp.exp(steps), shape[axis_at] // parts).reshape((-1,) + (1,) * (len(shape) - 1 - axis_at))
    return gain


def normal_values(stream_key, extent, deviation, reach, split=(), kind=jnp.bfloat16):
    entries = jax.random.normal(stream_key, extent, jnp.float32) * deviation
    if len(split) > 0:
        entries = block_scale(stream_key, extent, split, -0.22, 0.18) * entries
    return jnp.clip(entries, min=-reach, max=reach).astype(kind)


def setup_inputs(seed: int = 0, part: int = 0) -> dict:
    keys = jax.random.split(jax.random.key(seed), 5)
    part_splits = jax.random.split(jax.random.fold_in(keys[4], part), 5)
    return {
        "ancestor_inverse": normal_values(part_splits[0], (2, M, M), (SLOTS * BS) ** -0.5, 0.125, ((1, 4), (2, 4))),
        "panels": normal_values(part_splits[1], (NSUP, SLOTS * BS, 2 * W), 0.15, 0.8984375, ((1, 4),)),
        "block_lists": draw_block_lists(jax.random.fold_in(jax.random.fold_in(keys[4], part), 71), part),
        "diag_inverse": normal_values(part_splits[3], (NSUP, W, 2 * W), 1.0, 6.0, ((1, 16),), jnp.float32),
    }


def complex_product(left_real, left_imag, right):
    first = jnp.dot(left_real, right, preferred_element_type=jnp.float32)
    second = jnp.dot(left_imag, right, preferred_element_type=jnp.float32)
    return jnp.concatenate([first[:, :W] - second[:, W:], first[:, W:] + second[:, :W]], axis=1)


def reference(ancestor_inverse, panels, block_lists, diag_inverse):
    width = CAP * BS
    offdiag_all = []
    diag_all = []
    for k in range(NSUP):
        listed = block_lists[k]
        valid = (listed >= 0).astype(jnp.float32)
        row_index = (jnp.maximum(listed, 0)[:, None] * BS + jnp.arange(BS, dtype=jnp.int32)[None, :]).reshape(-1).astype(jnp.int32)
        row_mask = jnp.repeat(valid, BS)
        lhat = (panels[k].astype(jnp.float32) * row_mask[:, None]).astype(jnp.bfloat16)
        picked = jnp.take(jnp.take(ancestor_inverse, row_index, axis=1), row_index, axis=2)

        def add_range(total, range_id):
            columns = lax.dynamic_slice_in_dim(picked, range_id * width, width, 2)
            rows = lax.dynamic_slice_in_dim(lhat, range_id * width, width, 0)
            term = complex_product(columns[0], columns[1], rows) * row_mask[:, None]
            rounded = lax.optimization_barrier(term.astype(jnp.bfloat16))
            return total + rounded.astype(jnp.float32), None

        start = jnp.zeros((SLOTS * BS, 2 * W), jnp.float32)
        total, unused = lax.scan(add_range, start, jnp.arange(GRID, dtype=jnp.int32))
        offdiag = (-total).astype(jnp.bfloat16)
        update = complex_product(lhat[:, :W].T, lhat[:, W:].T, offdiag)
        offdiag_all.append(offdiag)
        diag_all.append(diag_inverse[k] - update)
    return jnp.stack(offdiag_all), jnp.stack(diag_all)
```

```python
import functools

import jax
import jax.numpy as jnp
from jax import lax
from jax.experimental import pallas as pl
from jax.experimental.pallas import tpu as pltpu
from jax.sharding import PartitionSpec as P

CAP = 4


BOTH = ("col", "row")


def range_senders(ncol, nrow):
    chips = max(nrow // 2, 1)
    load = {}
    pairs = []
    flows = [(r, c) for r in range(nrow) for c in range(ncol) if c != r]
    used = {r: set() for r in range(nrow)}
    for r, c in sorted(flows, key=lambda f: (-abs(f[0] - f[1]), f)):
        step = 1 if c > r else -1
        best = None
        for source in range(nrow):
            if source in used[r]:
                continue
            chip = source // 2 % chips
            path = [("col", chip, z, step) for z in range(r, c, step)]
            here, there = chip, r // 2 % chips
            turn = 1 if there > here else -1
            path += [("row", c, x, turn) for x in range(here, there, turn)]
            cost = (
                max(load.get(link, 0) for link in path),
                sum(load.get(link, 0) for link in path),
                abs(here - there),
                source,
            )
            if best is None or cost < best[0]:
                best = (cost, source, path)
        _, source, path = best
        used[r].add(source)
        for link in path:
            load[link] = load.get(link, 0) + 1
        pairs.append((r * nrow + source, c * nrow + r))
    return pairs


def complex_of(first, second):
    half = first.shape[1] // 2
    return jnp.concatenate(
        [first[:, :half] - second[:, half:], first[:, half:] + second[:, :half]], axis=1
    )


def product_kernel(k, nrow, lists, inverse, own, came, kept, sent, spread, total):
    here_col = lax.axis_index("col")
    here_row = lax.axis_index("row")
    low = here_row % 2
    bs = own.shape[1] // CAP
    bpr = inverse.shape[1] // bs
    spread[...] = jnp.zeros_like(spread)
    for s in range(CAP):
        block = lists[k, here_row * CAP + s]
        place = pl.ds(pl.multiple_of(jnp.clip(block - here_row * bpr, 0, bpr - 1) * bs, bs), bs)

        @pl.when((block >= 0) & (here_col == here_row))
        def _():
            spread[place, :] = own[0, s * bs : (s + 1) * bs, :]

        @pl.when((block >= 0) & (here_col != here_row))
        def _():
            spread[place, :] = came[s * bs : (s + 1) * bs, :]

    listed = spread[...]
    first = jnp.dot(inverse[0], listed, preferred_element_type=jnp.float32)
    second = jnp.dot(inverse[1], listed, preferred_element_type=jnp.float32)
    total[...] = complex_of(first, second)
    rows = CAP * bs // nrow
    for out, parity in ((kept, low), (sent, 1 - low)):
        for j in range(nrow // 2):
            at = (2 * j + parity) * rows
            block = lists[k, here_col * CAP + at // bs]
            start = jnp.clip(block - here_col * bpr, 0, bpr - 1) * bs + at % bs
            value = total[pl.ds(pl.multiple_of(start, rows), rows), :]
            out[j * rows : (j + 1) * rows, :] = jnp.where(block >= 0, value, 0.0).astype(out.dtype)


def product(k, nrow, lists, inverse, panels, came):
    _, rows, width = panels.shape
    half = jax.ShapeDtypeStruct((rows // 2, width), jnp.bfloat16)
    vmem = pl.BlockSpec(memory_space=pltpu.VMEM)
    return pl.pallas_call(
        functools.partial(product_kernel, k, nrow),
        out_shape=(half, half),
        grid=(1,),
        in_specs=[
            pl.BlockSpec(memory_space=pltpu.SMEM),
            vmem,
            pl.BlockSpec((1, rows, width), lambda i: (k, 0, 0)),
            vmem,
        ],
        out_specs=(vmem, vmem),
        scratch_shapes=[
            pltpu.VMEM((rows, width), jnp.bfloat16),
            pltpu.VMEM((rows, width), jnp.float32),
        ],
        cost_estimate=pl.CostEstimate(
            flops=4 * rows * rows * width, bytes_accessed=8 * rows * rows, transcendentals=0
        ),
        name=f"product_{k}",
    )(lists, inverse, panels, came)


def update_kernel(k, nrow, lists, kept, came, own, offdiag, update):
    here_col = lax.axis_index("col")
    here_row = lax.axis_index("row")
    block = lists[k, here_col * CAP + here_row * CAP // nrow]
    total = kept[...].astype(jnp.float32) + came[...].astype(jnp.float32)
    result = (-total).astype(offdiag.dtype)
    offdiag[...] = result
    listed = jnp.where(block >= 0, own[...].astype(jnp.float32), 0.0).astype(own.dtype)
    half = listed.shape[1] // 2
    dims = (((0,), (0,)), ((), ()))
    first = lax.dot_general(listed[:, :half], result, dims, preferred_element_type=jnp.float32)
    second = lax.dot_general(listed[:, half:], result, dims, preferred_element_type=jnp.float32)
    update[...] = complex_of(first, second).astype(update.dtype)


def update_of(k, nrow, lists, kept, came, own):
    rows, width = kept.shape
    vmem = pl.BlockSpec(memory_space=pltpu.VMEM)
    return pl.pallas_call(
        functools.partial(update_kernel, k, nrow),
        out_shape=(
            jax.ShapeDtypeStruct((rows, width), jnp.bfloat16),
            jax.ShapeDtypeStruct((width // 2, width), jnp.bfloat16),
        ),
        in_specs=[pl.BlockSpec(memory_space=pltpu.SMEM), vmem, vmem, vmem],
        out_specs=(vmem, vmem),
        cost_estimate=pl.CostEstimate(
            flops=2 * rows * width * width, bytes_accessed=4 * width * width, transcendentals=0
        ),
        name=f"update_{k}",
    )(lists, kept, came, own)


def swap(value, axis, size, bit):
    return lax.ppermute(value, axis, [(i, i ^ bit) for i in range(size)])


def halve(value, axis, size, bit):
    mine = (lax.axis_index(axis) // bit) % 2
    send = lax.dynamic_index_in_dim(value, 1 - mine, 1, keepdims=False)
    keep = lax.dynamic_index_in_dim(value, mine, 1, keepdims=False)
    got = swap(send, axis, size, bit)
    return (keep.astype(jnp.float32) + got.astype(jnp.float32)).astype(value.dtype)


def on_device(ncol, nrow, ancestor_inverse, panels, block_lists, diag_inverse):
    here_row = lax.axis_index("row")
    nsup, rows, width = panels.shape
    share = rows // nrow
    pairs = range_senders(ncol, nrow)
    own = lax.dynamic_slice_in_dim(panels, here_row * share, share, 1)
    came = [lax.ppermute(panels[k], BOTH, pairs) for k in range(nsup)]
    offdiag, updates = [], []
    for k in range(nsup):
        kept, sent = product(k, nrow, block_lists, ancestor_inverse, panels, came[k])
        got = swap(sent, "row", nrow, 1)
        value = (kept.astype(jnp.float32) + got.astype(jnp.float32)).astype(jnp.bfloat16)
        bit = 2
        while bit < nrow // 2:
            value = value.reshape(nrow // (2 * bit), 2, share, width)
            value = halve(value, "row", nrow, bit).reshape(-1, width)
            bit *= 2
        mine = (here_row // bit) % 2
        value = value.reshape(2, share, width)
        send = lax.dynamic_index_in_dim(value, 1 - mine, 0, keepdims=False)
        keep = lax.dynamic_index_in_dim(value, mine, 0, keepdims=False)
        got = swap(send, "row", nrow, bit)
        result, update = update_of(k, nrow, block_lists, keep, got, own[k])
        offdiag.append(result)
        updates.append(update)
    outs = []
    for k in range(nsup):
        value = updates[k]
        per = value.shape[0] // (ncol * nrow)
        bit = 1
        left = nrow
        while bit < nrow:
            left //= 2
            value = value.reshape(ncol * left, 2, per, width)
            value = halve(value, "row", nrow, bit)
            bit *= 2
        value = value.reshape(ncol, per, width)
        total = lax.dynamic_index_in_dim(value, lax.axis_index("col"), 0, keepdims=False)
        total = total.astype(jnp.float32)
        for d in range(1, ncol):
            other = (lax.axis_index("col") + d) % ncol
            send = lax.dynamic_index_in_dim(value, other, 0, keepdims=False)
            got = lax.ppermute(send, "col", [(i, (i + d) % ncol) for i in range(ncol)])
            total = total + got.astype(jnp.float32)
        outs.append(total)
    return jnp.stack(offdiag), diag_inverse - jnp.stack(outs)


def solution(mesh):
    sizes = (mesh.shape["col"], mesh.shape["row"])
    return jax.shard_map(
        functools.partial(on_device, *sizes),
        mesh=mesh,
        in_specs=(
            P("pole", "col", "row"),
            P("pole", "col", None),
            P("pole", None),
            P("pole", ("col", "row"), None),
        ),
        out_specs=(P("pole", ("col", "row"), None), P("pole", ("col", "row"), None)),
        check_vma=False,
    )
```
